32 devices in a mesh: groups: 2 (over x), tm: 8 (over z, y), video: 2 (over core).
Axes of the slice: x: 2, y: 2, z: 4, core: 2. Of those that a mesh axis runs over, the one named last changes fastest.
Arguments:
- queries: bfloat16 [8, 896, 512], P(('groups', 'video'), 'tm'), parts along dimension 0, may hold values from -80 to 80
- query_lengths: int32 [8], P(('groups', 'video')), parts along dimension 0, may hold values from 224 to 896
- bank: bfloat16 [512, 512, 512], P(('groups', 'video'), 'tm'), parts along dimension 0, may hold values from -80 to 80
- ref_lengths: int32 [512], P('groups'), parts along dimension 0, may hold values from 128 to 512
- owner_map: int32 [512], P('groups'), parts along dimension 0, may hold values from 0 to 255, each once
- candidates: int32 [8, 8], P('groups'), parts along dimension 0, may hold values from 0 to 255
Outputs:
- match_score: float32 [8, 8, 512], P(('groups', 'video'), None, 'tm'), parts along dimension 0
- aligned_time: float32 [8, 8, 512], P(('groups', 'video'), None, 'tm'), parts along dimension 0
The draws below stay inside these ranges and needn't reach their ends.
There are 2 independent parts, one for each index of `groups`. The reference program is written for one: setup_inputs(seed, part) draws one part's arguments, and reference() takes and returns one part's arrays. A program takes and returns all parts, laid end to end along the dimension named above; each array names one. Nothing has to cross between parts.
All inputs are finite; a program needn't handle non-finite values.
Results may differ from the reference program's by a relative error of at most 0.0003.
Values may be sent and summed in bfloat16 or wider, within the bound.
No kernel may reach another device: no remote copies, remote signals or barrier semaphores. Data moves between devices by JAX's collectives and lax.ppermute only.
A program may use at most 64 MiB of HBM per device.

```python
import math
import jax
import jax.numpy as jnp
import numpy as np
from jax import lax

E = 512
CAND = 8
RT = 512
QV = 4
QT = 896
NREF = 256


def spiked(key, shape):
    base = jnp.clip(jax.random.normal(key, shape, jnp.float32), -6.0, 6.0)
    return base


def draw_queries(key, part):
    return spiked(key, (QV, QT, E)).astype(jnp.bfloat16)


def draw_bank(key, part):
    return spiked(key, (NREF, RT, E)).astype(jnp.bfloat16)


def set_ends(values, rng, low, largest):
    spot = [jax.random.randint(jax.random.fold_in(rng, axis), (), 0, length) for axis, length in enumerate(values.shape)]
    longest = values.shape.index(max(values.shape))
    neighbour = spot[:longest] + [(spot[longest] + 1) % values.shape[longest]] + spot[longest + 1:]
    return values.at[tuple(spot)].set(low).at[tuple(neighbour)].set(largest)


def rank_bounds(amount, skew):
    loads = [(1 << 20) // math.isqrt(grade ** skew) + 1 for grade in range(1, amount + 1)]
    scale = 1 + sum(loads) // (1 << 30)
    return np.cumsum(np.array([max(1, weight // scale) for weight in loads]))


def skewed_ids(rng, dims, count, slope):
    listing = rank_bounds(count, slope)
    lot = jax.random.randint(jax.random.fold_in(rng, 1), dims, 0, int(listing[count - 1]))
    standing = jnp.searchsorted(jnp.asarray(listing, jnp.int32), lot, side="right")
    return jax.random.permutation(jax.random.fold_in(rng, 2), count)[standing].astype(jnp.int32)


def setup_inputs(seed: int = 0, part: int = 0) -> dict:
    arg_keys = jax.random.split(jax.random.key(seed), 7)
    own_keys = jax.random.split(jax.random.fold_in(arg_keys[6], part), 7)
    queries = draw_queries(jax.random.fold_in(jax.random.fold_in(arg_keys[6], part), 71), part)
    query_lengths = set_ends(jax.random.randint(own_keys[1], (QV,), QT // 4, QT + 1), jax.random.fold_in(own_keys[1], 1), QT // 4, QT).astype(jnp.int32)
    bank = draw_bank(jax.random.fold_in(jax.random.fold_in(arg_keys[6], part), 71), part)
    ref_lengths = set_ends(jax.random.randint(own_keys[3], (NREF,), RT // 4, RT + 1), jax.random.fold_in(own_keys[3], 1), RT // 4, RT).astype(jnp.int32)
    owner_map = jax.random.permutation(own_keys[4], NREF).astype(jnp.int32)
    candidates = set_ends(skewed_ids(own_keys[5], (QV, CAND), NREF, 2), jax.random.fold_in(own_keys[5], 3), 0, NREF - 1).astype(jnp.int32)
    return dict(queries=queries, query_lengths=query_lengths, bank=bank, ref_lengths=ref_lengths, owner_map=owner_map, candidates=candidates)


SHARPNESS = 10.0
NEG_FLOOR = -1e+30

def reference(queries, query_lengths, bank, ref_lengths, owner_map, candidates):
    total_q = queries.shape[1]
    width = queries.shape[2]
    ref_total = bank.shape[1]
    query_live = jnp.arange(total_q, dtype=jnp.int32)[None, :] < query_lengths[:, None]
    masked = jnp.where(query_live[:, :, None], queries, jnp.zeros_like(queries))
    row_ids = owner_map[candidates].astype(jnp.int32)
    ref_len = ref_lengths[candidates]
    ref_live = jnp.arange(ref_total, dtype=jnp.int32)[None, None, :] < ref_len[:, :, None]
    position = jnp.arange(total_q, dtype=jnp.float32) / total_q

    def per_video(inputs):
        frames, rows_here, live, rlive = inputs
        refs = bank[rows_here]
        refs = jnp.where(rlive[:, :, None], refs, jnp.zeros_like(refs))
        scores = jnp.einsum('qe,cre->cqr', frames.astype(jnp.float32), refs.astype(jnp.float32), precision=lax.Precision.HIGHEST) / math.sqrt(width)
        widened = jnp.pad(scores, ((0, 0), (4, 4), (4, 4)))
        filtered = widened[:, 0:total_q, 0:ref_total]
        for offset in range(1, 9):
            filtered = filtered + widened[:, offset:offset + total_q, offset:offset + ref_total]
        filtered = filtered / 9.0
        logits = SHARPNESS * filtered
        live_b = live[None, :, None]
        top = lax.optimization_barrier(jnp.max(jnp.where(live_b, logits, NEG_FLOOR), axis=1))
        weights = jnp.where(live_b, jnp.exp(logits - top[:, None, :]), 0.0)
        total = lax.optimization_barrier(jnp.sum(weights, axis=1))
        score = lax.optimization_barrier(jnp.sum(weights * filtered, axis=1)) / total
        aligned = lax.optimization_barrier(jnp.sum(weights * position[None, :, None], axis=1)) / total
        factor = rlive.astype(jnp.float32)
        return (score * factor, aligned * factor)
    return lax.map(per_video, (masked, row_ids, query_live, ref_live))
```

```python
import math

import jax
import jax.numpy as jnp
from jax import lax
from jax.experimental import pallas as pl
from jax.experimental.pallas import tpu as pltpu
from jax.sharding import PartitionSpec as P

SHARPNESS = 10.0
NEG_FLOOR = -1e30
REACH = 4
TAPS = 2 * REACH + 1
LANES = 128
SUB = 8
LOG2E = math.log2(math.e)


def table_lookup(indices, table):
    onehot = indices[..., None] == jnp.arange(table.shape[0], dtype=jnp.int32)
    return jnp.sum(jnp.where(onehot, table, 0), axis=-1)


def ring_order(count):
    return list(range(0, count, 2)) + list(range(count - 1 - count % 2, 0, -2))


def ring_place(index, count):
    return jnp.where(index % 2 == 0, index // 2, count - 1 - index // 2)


def ring_member(place, count):
    place = lax.rem(place + 2 * count, count)
    return jnp.where(place < (count + 1) // 2, 2 * place, 2 * (count - 1 - place) + 1)


def padded(n, to):
    return -(-n // to) * to


def filtered_planes(load, planes, lanes):
    turned, pairs, quads = {}, {}, {}
    for m in range(planes + TAPS - 1):
        turned[m] = pltpu.roll(load(m), (lanes - m) % lanes, 1) if m % lanes else load(m)
        if m >= 1:
            pairs[m - 1] = turned[m - 1] + turned[m]
        if m >= 3:
            quads[m - 3] = pairs[m - 3] + pairs[m - 1]
        if m >= 8:
            i = m - 8
            total = quads[i] + quads[i + 4] + turned[m]
            yield i, pltpu.roll(total, (i + REACH) % lanes, 1)


def block_stats(dims, refs_ref, passes, s_ref, lg_ref, out):
    planes, lanes, cand, scale, total_frames = dims
    lane = lax.broadcasted_iota(jnp.int32, (SUB, lanes), 1)
    wheres = []
    for k, (block, live, valid, frame) in enumerate(passes):
        cols = block.shape[0]
        s_ref[:, :cols] = lax.dot_general(
            refs_ref, block, (((1,), (1,)), ((), ())), preferred_element_type=jnp.float32
        )
        ok = valid & (live > lane)

        def load(m, live=live):
            return jnp.where(live > lane, s_ref[m * SUB : (m + 1) * SUB, :], 0.0)

        for i, f in filtered_planes(load, planes, lanes):
            lg_ref[k, i * SUB : (i + 1) * SUB, :] = jnp.where(ok, f * scale, NEG_FLOOR)
        wheres.append(frame.astype(jnp.float32) / total_frames)
    for i in range(planes):
        rows = slice(i * SUB, (i + 1) * SUB)
        logits = [lg_ref[k, rows, :] for k in range(len(passes))]
        top = logits[0]
        for l in logits[1:]:
            top = jnp.maximum(top, l)
        total = score = moment = None
        for l, w in zip(logits, wheres):
            e = jnp.exp2(l - top)
            if total is None:
                total, score, moment = e, e * l, e * w
            else:
                total, score, moment = total + e, score + e * l, moment + e * w
        out(rows, top, total, score, moment)


def shard_pass(block, shard, count, frames, length, lane):
    live = jnp.minimum(length - shard * frames, frames)
    low = jnp.where(shard > 0, REACH, 0)
    high = jnp.where(shard < count - 1, frames - REACH, frames)
    return block, live, (lane >= low) & (lane < high), shard * frames + lane


def stats_kernel(cfg, members, *args):
    count, frames, dims = cfg
    n = len(members)
    refs_ref, lens_ref = args[0], args[1]
    q_refs = args[2 : 2 + n]
    stat_ref = args[2 + n]
    s_ref, lg_ref = args[3 + n :]
    place = ring_place(lax.axis_index("tm"), count)
    lane = lax.broadcasted_iota(jnp.int32, (SUB, dims[1]), 1)

    def video(v, carry):
        passes = []
        for ref, hop in zip(q_refs, members):
            shard = ring_member(place + hop, count)
            passes.append(shard_pass(ref[v], shard, count, frames, lens_ref[v], lane))

        def out(rows, *stats):
            for j, x in enumerate(stats):
                stat_ref[j, v, rows, :] = x

        block_stats(dims, refs_ref[v], passes, s_ref, lg_ref, out)
        return carry

    lax.fori_loop(0, stat_ref.shape[1], video, 0)


def final_kernel(cfg, members, far_split, prior, *args):
    count, frames, dims = cfg
    planes, lanes, cand, scale, total_frames = dims
    n = len(members)
    refs_ref, lens_ref, factor_ref = args[0], args[1], args[2]
    q_refs = args[3 : 3 + n]
    far_refs = args[3 + n : 3 + n + len(far_split)]
    rest = args[3 + n + len(far_split) :]
    prior_refs = rest[:prior]
    score_ref, time_ref = rest[prior : prior + 2]
    s_ref, lg_ref, edge_ref, st_ref, far_ref = rest[prior + 2 :]
    place = ring_place(lax.axis_index("tm"), count)
    lane = lax.broadcasted_iota(jnp.int32, (SUB, lanes), 1)
    far = ring_member(place + count // 2, count)
    videos = score_ref.shape[0]
    start = 0
    for ref, size in zip(far_refs, far_split):
        far_ref[start : start + size] = ref[...]
        start += size
    group = lanes // (4 * REACH)
    blocks = -(-(count - 1) // group)

    def video(v, carry):
        every = [(q_refs[k], ring_member(place + hop, count)) for k, hop in enumerate(members)]
        every.append((far_ref, far))
        half = 2 * REACH
        for ref, shard in every:
            at = pl.multiple_of(shard * 2 * half, half)
            edge_ref[pl.ds(at, half), :] = ref[v, :half, :].astype(jnp.float32)
            edge_ref[pl.ds(at + half, half), :] = ref[v, frames - half :, :].astype(jnp.float32)
        passes = [shard_pass(far_ref[v], far, count, frames, lens_ref[v], lane)]
        w = lane % (2 * half)
        for b in range(blocks):
            first = half + b * lanes
            bound = b * group + 1 + lane // (2 * half)
            frame = bound * frames - half + w
            valid = (w >= REACH) & (w < half + REACH) & (bound < count) & (frame < lens_ref[v])
            rows = min(lanes, (count - 1 - b * group) * 2 * half)
            edge = edge_ref[first : first + rows, :].astype(jnp.bfloat16)
            passes.append((edge, frame, valid, lens_ref[v], rows))

        def out(rows, *stats):
            for j, x in enumerate(stats):
                st_ref[j, rows, :] = x

        wheres = []
        for k, item in enumerate(passes):
            if len(item) == 4:
                block, live, valid, frame = item
                alive = lane < live
                ok = valid & alive
            else:
                block, frame, ok, length, rows = item
                alive = (frame < length) & (lane < rows)
            s_ref[:, : block.shape[0]] = lax.dot_general(
                refs_ref[v], block, (((1,), (1,)), ((), ())), preferred_element_type=jnp.float32
            )

            def load(m, alive=alive):
                return jnp.where(alive, s_ref[m * SUB : (m + 1) * SUB, :], 0.0)

            for i, f in filtered_planes(load, planes, lanes):
                lg_ref[k, i * SUB : (i + 1) * SUB, :] = jnp.where(ok, f * scale, NEG_FLOOR)
            wheres.append(frame.astype(jnp.float32) / total_frames)
        tot = jnp.ones((SUB, lanes), jnp.float32)
        sco = jnp.zeros((SUB, lanes), jnp.float32)
        mom = jnp.zeros((SUB, lanes), jnp.float32)
        for i in range(planes):
            rows = slice(i * SUB, (i + 1) * SUB)
            logits = [lg_ref[k, rows, :] for k in range(len(passes))]
            tops = [ref[0, v, rows, :] for ref in prior_refs]
            top = logits[0]
            for l in logits[1:] + tops:
                top = jnp.maximum(top, l)
            top = jnp.max(top, axis=1, keepdims=True)
            total = score = moment = 0.0
            for l, where in zip(logits, wheres):
                e = jnp.exp2(l - top)
                total, score, moment = total + e, score + e * l, moment + e * where
            for ref, t in zip(prior_refs, tops):
                e = jnp.exp2(t - top)
                total += e * ref[1, v, rows, :]
                score += e * ref[2, v, rows, :]
                moment += e * ref[3, v, rows, :]
            here = lane == i
            tot = jnp.where(here, jnp.sum(total, axis=1, keepdims=True), tot)
            sco = jnp.where(here, jnp.sum(score, axis=1, keepdims=True), sco)
            mom = jnp.where(here, jnp.sum(moment, axis=1, keepdims=True), mom)
        factor = factor_ref[v]
        score_ref[v] = (sco / tot * (1.0 / (SHARPNESS * LOG2E)))[:cand, :planes] * factor
        time_ref[v] = (mom / tot)[:cand, :planes] * factor
        return carry

    lax.fori_loop(0, videos, video, 0)


def on_device(queries, query_lengths, bank, ref_lengths, owner_map, candidates):
    video_count = lax.axis_size("video")
    video_index = lax.axis_index("video")
    count = lax.axis_size("tm")
    time_index = lax.axis_index("tm")
    videos, frames, width = queries.shape
    owned_rows, ref_here, _ = bank.shape
    cand = candidates.shape[1]
    total_frames = frames * count

    order = ring_order(count)
    up = [(order[i], order[(i + 1) % count]) for i in range(count)]
    down = [(b, a) for a, b in up]
    slots = [(queries, 0)]
    fwd = bwd = queries
    for hop in range(1, count // 2):
        fwd = lax.ppermute(fwd, "tm", up)
        bwd = lax.ppermute(bwd, "tm", down)
        slots += [(fwd, -hop), (bwd, hop)]
    cut = (videos + 1) // 2
    far = [lax.ppermute(fwd[:cut], "tm", up)]
    if cut < videos:
        far.append(lax.ppermute(bwd[cut:], "tm", down))

    grouped = candidates.reshape(video_count, videos * cand)
    bank_rows = table_lookup(grouped, owner_map)
    local_rows = bank_rows - video_index * owned_rows
    owned = (local_rows >= 0) & (local_rows < owned_rows)
    picked = jnp.take(bank, jnp.clip(local_rows, 0, owned_rows - 1), axis=0)
    outgoing = jnp.where(owned[:, :, None, None], picked, jnp.zeros_like(picked))
    arrived = lax.all_to_all(outgoing, "video", split_axis=0, concat_axis=0, tiled=True)
    fetched = jnp.sum(arrived, axis=0).reshape(videos, cand, ref_here, width)
    mine = lax.dynamic_slice_in_dim(candidates, video_index * videos, videos, 0)
    ref_len = table_lookup(mine, ref_lengths)
    ref_frame = time_index * ref_here + jnp.arange(ref_here, dtype=jnp.int32)
    ref_live = ref_frame[None, None, :] < ref_len[:, :, None]
    fetched = jnp.where(ref_live[..., None], fetched, jnp.zeros_like(fetched))
    line = [(i, i + 1) for i in range(count - 1)]
    low = lax.ppermute(fetched[:, :, ref_here - REACH :], "tm", line)
    high = lax.ppermute(fetched[:, :, :REACH], "tm", [(b, a) for a, b in line])
    near = jnp.concatenate([low, fetched, high], axis=2)
    near = jnp.pad(near, ((0, 0), (0, padded(cand, SUB) - cand), (0, 0), (0, 0)))
    refs = near.transpose(0, 2, 1, 3).reshape(videos, (ref_here + 2 * REACH) * SUB, width)
    factor = ref_live.astype(jnp.float32)

    lanes = padded(frames + 2 * REACH, LANES)
    scale = SHARPNESS * LOG2E / (TAPS * math.sqrt(width))
    dims = (ref_here, lanes, cand, scale, total_frames)
    cfg = (count, frames, dims)
    rows = ref_here * SUB
    vmem = pl.BlockSpec(memory_space=pltpu.VMEM)
    smem = pl.BlockSpec(memory_space=pltpu.SMEM)
    score_rows = pltpu.VMEM((refs.shape[1], lanes), jnp.float32)

    def stats(part, name):
        n = len(part)
        return pl.pallas_call(
            lambda *a: stats_kernel(cfg, [hop for _, hop in part], *a),
            out_shape=jax.ShapeDtypeStruct((4, videos, rows, lanes), jnp.float32),
            in_specs=[vmem, smem] + [vmem] * n,
            out_specs=vmem,
            scratch_shapes=[score_rows, pltpu.VMEM((n, rows, lanes), jnp.float32)],
            compiler_params=pltpu.CompilerParams(vmem_limit_bytes=24 * 2**20),
            cost_estimate=pl.CostEstimate(
                flops=2 * n * videos * refs.shape[1] * width * lanes,
                bytes_accessed=n * videos * rows * lanes * 4,
                transcendentals=n * videos * rows * lanes,
            ),
            name=name,
        )(refs, query_lengths, *[q for q, _ in part])

    late = 2 if count > 4 else 0
    parts = [slots[: len(slots) - late]] + ([slots[-late:]] if late else [])
    prior = [stats(part, f"stats{k}") for k, part in enumerate(parts)]
    edges = 2 * (2 * REACH) * count
    passes = 1 + -(-(count - 1) // (lanes // (4 * REACH)))
    return pl.pallas_call(
        lambda *a: final_kernel(
            cfg, [hop for _, hop in slots], [f.shape[0] for f in far], len(prior), *a
        ),
        out_shape=[jax.ShapeDtypeStruct((videos, cand, ref_here), jnp.float32)] * 2,
        in_specs=[vmem, smem, vmem] + [vmem] * (len(slots) + len(far) + len(prior)),
        out_specs=[vmem, vmem],
        scratch_shapes=[
            score_rows,
            pltpu.VMEM((passes, rows, lanes), jnp.float32),
            pltpu.VMEM((padded(edges, LANES) + LANES, width), jnp.float32),
            pltpu.VMEM((4, rows, lanes), jnp.float32),
            pltpu.VMEM((videos, frames, width), jnp.bfloat16),
        ],
        compiler_params=pltpu.CompilerParams(vmem_limit_bytes=32 * 2**20),
        name="finish",
    )(refs, query_lengths, factor, *[q for q, _ in slots], *far, *prior)


def solution(mesh):
    return jax.shard_map(
        on_device,
        mesh=mesh,
        in_specs=(
            P(("groups", "video"), "tm", None),
            P(("groups", "video")),
            P(("groups", "video"), "tm", None),
            P("groups"),
            P("groups"),
            P("groups", None),
        ),
        out_specs=(P(("groups", "video"), None, "tm"), P(("groups", "video"), None, "tm")),
        check_vma=False,
    )
```
